32 devices in a mesh: parts: 2 (over y), dp: 4 (over z), section: 2 (over x), chan: 2 (over core).
Axes of the slice: x: 2, y: 2, z: 4, core: 2. Of those that a mesh axis runs over, the one named last changes fastest.
Arguments:
- block_inputs: bfloat16 [2, 16, 8, 8, 1024], P('section', ('parts', 'dp')), parts along dimension 1, may hold values from -6 to 6
- out_pre: bfloat16 [2, 16, 8, 8, 1024], P('section', ('parts', 'dp')), parts along dimension 1, may hold values from -6 to 6
- first_pre: bfloat16 [2, 16, 8, 8, 1024], P('section', ('parts', 'dp'), None, None, 'chan'), parts along dimension 1, may hold values from -6 to 6
- second_pre: bfloat16 [2, 16, 8, 8, 1024], P('section', ('parts', 'dp'), None, None, 'chan'), parts along dimension 1, may hold values from -6 to 6
- w_reduce: bfloat16 [2, 1024, 1024], P('section', None, 'chan'), may hold values from -0.1875 to 0.1875
- w_group: bfloat16 [2, 9, 64, 16, 16], P('section', None, 'chan'), may hold values from -0.5 to 0.5
- w_expand: bfloat16 [2, 1024, 1024], P('section', 'chan'), may hold values from -0.1875 to 0.1875
- w_lateral: bfloat16 [1024, 256], replicated, may hold values from -0.1875 to 0.1875
- teacher: bfloat16 [16, 8, 8, 256], P(('parts', 'dp')), parts along dimension 0, may hold values from -6 to 6
- top_grad: bfloat16 [16, 8, 8, 1024], P(('parts', 'dp')), parts along dimension 0, may hold values from -6 to 6
- boxes: int32 [16, 8, 4], P(('parts', 'dp')), parts along dimension 0, may hold values from 0 to 8, as said below
- region_counts: int32 [16], P(('parts', 'dp')), parts along dimension 0, may hold values from 1 to 8
Outputs:
- input_grads: bfloat16 [2, 16, 8, 8, 1024], P('section', ('parts', 'dp')), parts along dimension 1
- reduce_grads: float32 [4, 1024, 1024], P(('parts', 'section'), 'dp', 'chan'), parts along dimension 0
- group_grads: float32 [4, 9, 64, 16, 16], P(('parts', 'section'), None, 'chan', 'dp'), parts along dimension 0
- expand_grads: float32 [4, 1024, 1024], P(('parts', 'section'), 'chan', 'dp'), parts along dimension 0
The draws below stay inside these ranges and needn't reach their ends.
There are 2 independent parts, one for each index of `parts`. The reference program is written for one: setup_inputs(seed, part) draws one part's arguments, and reference() takes and returns one part's arrays. A program takes and returns all parts, laid end to end along the dimension named above; an argument that names none is the same for every part. Nothing has to cross between parts.
Inputs may be any that keep to these rules, and one draw needn't show every extreme that they name: `boxes`: each used row is a region with top < bottom and left < right; only the first region_counts[i] rows of page i are used, the others are padding.
All inputs are finite; a program needn't handle non-finite values.
Results may differ from the reference program's by a relative error of at most 0.0059.
Values may be sent and summed in bfloat16 or wider, within the bound.
A program may use at most 128 MiB of HBM per device.

```python
import math
import jax
import jax.numpy as jnp
from jax import lax

C = 1024
G = 64
GW = 16
LAT = 256
SIDE = 8
R_MAX = 8
IMAGES = 8
PIXELS = 512
BLOCKS = 2


def draw_boxes(key, part):
    height_key, width_key, top_key, left_key = jax.random.split(jax.random.fold_in(key, 11), 4)
    page_index = jnp.arange(IMAGES, dtype=jnp.int32)
    largest = jnp.maximum(1, SIDE * (IMAGES + 2 * page_index) // (3 * IMAGES))[:, None]
    height = jax.random.randint(height_key, (IMAGES, R_MAX), 1, largest + 1)
    width = jax.random.randint(width_key, (IMAGES, R_MAX), 1, largest + 1)
    top_edge = jax.random.randint(top_key, (IMAGES, R_MAX), 0, SIDE - height + 1)
    left_edge = jax.random.randint(left_key, (IMAGES, R_MAX), 0, SIDE - width + 1)
    layout = jnp.stack([top_edge, top_edge + height, left_edge, left_edge + width], axis=-1)
    whole_page = jnp.array([0, SIDE, 0, SIDE], dtype=jnp.int32)
    layout = layout.at[IMAGES - 1, 0].set(whole_page)
    return layout.astype(jnp.int32)


def draw_region_counts(key, part):
    counts = jax.random.randint(jax.random.fold_in(key, 23), (IMAGES,), 1, R_MAX + 1)
    counts = counts.at[0].set(R_MAX)
    counts = counts.at[IMAGES - 1].set(1)
    return counts.astype(jnp.int32)


def raised(values, rng, source, target, parts, factor):
    owner, partner = [(jnp.arange(values.shape[dim]) // (values.shape[dim] // parts)).reshape([-1 if axis == dim else 1 for axis in range(values.ndim)]) for dim in (source, target)]
    chosen = jax.random.permutation(rng, parts)[partner]
    strong = (owner == chosen) | (owner == (partner + parts // 2) % parts)
    return jnp.where(strong, factor * values, values)


def steps_of(stream_key, dims, cuts, smallest, top_value):
    def one(dim, blocks):
        steps = jax.random.uniform(jax.random.fold_in(jax.random.fold_in(stream_key, 6), dim), (blocks,), jnp.float32, smallest / len(cuts), top_value / len(cuts))
        return jnp.repeat(jnp.exp(steps), dims[dim] // blocks).reshape((-1,) + (1,) * (len(dims) - dim - 1))

    loudness = one(*cuts[0])
    for cut in cuts[1:]:
        loudness = loudness * one(*cut)
    return loudness


def centred(rng, dims, scale, most, cuts=(), kind=jnp.bfloat16):
    values = jax.random.normal(rng, dims, jnp.float32) * scale
    if len(cuts) > 0:
        values = steps_of(rng, dims, cuts, -0.22, 0.18) * values
    return jnp.clip(values, min=-most, max=most).astype(kind)


def gaussian_with(own_key, shape, deviation, reach, cuts, heavy, kind=jnp.bfloat16):
    result = deviation * jax.random.normal(own_key, shape, jnp.float32)
    if cuts:
        result = result * steps_of(own_key, shape, cuts, -0.22, 0.18)
    return jnp.clip(raised(result, jax.random.fold_in(own_key, 3), *heavy), -reach, reach).astype(kind)


def setup_inputs(seed: int = 0, part: int = 0) -> dict:
    keys = jax.random.split(jax.random.key(seed), 13)
    part_splits = jax.random.split(jax.random.fold_in(keys[12], part), 13)
    block_inputs = gaussian_with(part_splits[0], (BLOCKS, IMAGES, SIDE, SIDE, C), 1.0, 6.0, ((0, 2), (1, 4)), (1, 4, 4, 2.0))
    out_pre = centred(part_splits[1], (BLOCKS, IMAGES, SIDE, SIDE, C), 1.0, 6.0, ((0, 2), (1, 4)))
    first_pre = centred(part_splits[2], (BLOCKS, IMAGES, SIDE, SIDE, C), 1.0, 6.0, ((0, 2), (1, 4), (4, 2)))
    second_pre = centred(part_splits[3], (BLOCKS, IMAGES, SIDE, SIDE, C), 1.0, 6.0, ((0, 2), (1, 4), (4, 2)))
    w_reduce = centred(keys[4], (BLOCKS, C, C), C ** -0.5, 0.1875, ((0, 2), (2, 2)))
    w_group = centred(keys[5], (BLOCKS, 9, G, GW, GW), (9 * GW) ** -0.5, 0.5, ((0, 2), (2, 2)))
    w_expand = centred(keys[6], (BLOCKS, C, C), C ** -0.5, 0.1875, ((0, 2), (1, 2)))
    w_lateral = centred(keys[7], (C, LAT), C ** -0.5, 0.1875)
    teacher = centred(part_splits[8], (IMAGES, SIDE, SIDE, LAT), 1.0, 6.0, ((0, 4),))
    top_grad = centred(part_splits[9], (IMAGES, SIDE, SIDE, C), 1.0, 6.0, ((0, 4),))
    boxes = draw_boxes(jax.random.fold_in(jax.random.fold_in(keys[12], part), 71), part)
    region_counts = draw_region_counts(jax.random.fold_in(jax.random.fold_in(keys[12], part), 71), part)
    return {"block_inputs": block_inputs, "out_pre": out_pre, "first_pre": first_pre, "second_pre": second_pre, "w_reduce": w_reduce, "w_group": w_group, "w_expand": w_expand, "w_lateral": w_lateral, "teacher": teacher, "top_grad": top_grad, "boxes": boxes, "region_counts": region_counts}


imitation_weight = 0.5
tap_offsets = [(tap_index // 3 - 1, tap_index % 3 - 1) for tap_index in range(9)]

def region_mask(boxes, region_counts):
    cells = jnp.arange(SIDE, dtype=jnp.int32)
    row_inside = (cells[None, None, :] >= boxes[:, :, 0:1]) & (cells[None, None, :] < boxes[:, :, 1:2])
    col_inside = (cells[None, None, :] >= boxes[:, :, 2:3]) & (cells[None, None, :] < boxes[:, :, 3:4])
    used = jnp.arange(R_MAX, dtype=jnp.int32)[None, :] < region_counts[:, None]
    inside = row_inside[:, :, :, None] & col_inside[:, :, None, :] & used[:, :, None, None]
    return jnp.any(inside, axis=1).astype(jnp.float32)

def reference(block_inputs, out_pre, first_pre, second_pre, w_reduce, w_group, w_expand, w_lateral, teacher, top_grad, boxes, region_counts):
    page_mask = region_mask(boxes, region_counts).reshape(-1, 1)
    covered = jnp.sum(page_mask)
    feature = jnp.maximum(out_pre[BLOCKS - 1], 0).reshape(-1, C)
    lateral = jnp.dot(feature, w_lateral, preferred_element_type=jnp.float32)
    error = (page_mask * (lateral - teacher.reshape(-1, LAT).astype(jnp.float32)) * (imitation_weight * PIXELS / covered)).astype(jnp.bfloat16)
    imitation = jnp.dot(error, w_lateral.T, preferred_element_type=jnp.float32)
    cotangent = (top_grad.reshape(-1, C).astype(jnp.float32) + imitation).astype(jnp.bfloat16)
    highest = lax.Precision.HIGHEST
    input_list, reduce_list, group_list, expand_list = ([], [], [], [])
    for block in range(BLOCKS - 1, -1, -1):
        out_rows = out_pre[block].reshape(-1, C)
        passed = jnp.where(out_rows > 0, cotangent, jnp.zeros_like(cotangent))
        second_rows = second_pre[block].reshape(-1, C)
        second_full = jnp.dot(passed, w_expand[block].T, preferred_element_type=jnp.float32)
        d_second = jnp.where(second_rows > 0, second_full, jnp.zeros_like(second_full)).astype(jnp.bfloat16)
        expand_sum = jnp.dot(jnp.maximum(second_rows, 0).T, passed, preferred_element_type=jnp.float32)
        relu_first = jnp.maximum(first_pre[block], 0).astype(jnp.float32).reshape(IMAGES, SIDE, SIDE, G, GW)
        padded_first = jnp.pad(relu_first, ((0, 0), (1, 1), (1, 1), (0, 0), (0, 0)))
        second_grid = d_second.astype(jnp.float32).reshape(IMAGES, SIDE, SIDE, G, GW)
        padded_second = jnp.pad(second_grid, ((0, 0), (1, 1), (1, 1), (0, 0), (0, 0)))
        group_weight = w_group[block].astype(jnp.float32)
        first_grad = jnp.zeros((IMAGES, SIDE, SIDE, G, GW), jnp.float32)
        group_terms = []
        for tap_index, (row_shift, col_shift) in enumerate(tap_offsets):
            shifted = padded_first[:, 1 + row_shift:1 + row_shift + SIDE, 1 + col_shift:1 + col_shift + SIDE]
            group_terms.append(jnp.einsum('nhwgi,nhwgo->gio', shifted, second_grid, precision=highest))
            behind = padded_second[:, 1 - row_shift:1 - row_shift + SIDE, 1 - col_shift:1 - col_shift + SIDE]
            first_grad = first_grad + jnp.einsum('nhwgo,gio->nhwgi', behind, group_weight[tap_index], precision=highest)
        first_rows = first_pre[block].reshape(-1, C)
        first_flat = first_grad.reshape(-1, C)
        d_first = jnp.where(first_rows > 0, first_flat, jnp.zeros_like(first_flat)).astype(jnp.bfloat16)
        reduce_sum = jnp.dot(block_inputs[block].reshape(-1, C).T, d_first, preferred_element_type=jnp.float32)
        cotangent = (jnp.dot(d_first, w_reduce[block].T, preferred_element_type=jnp.float32) + passed.astype(jnp.float32)).astype(jnp.bfloat16)
        input_list.append(cotangent.reshape(IMAGES, SIDE, SIDE, C))
        reduce_list.append(reduce_sum)
        group_list.append(jnp.stack(group_terms))
        expand_list.append(expand_sum)
    scale = 1.0 / math.sqrt(PIXELS)
    input_grads = jnp.stack(input_list[::-1])
    reduce_grads = jnp.stack(reduce_list[::-1]) * scale
    group_grads = jnp.stack(group_list[::-1]) * scale
    expand_grads = jnp.stack(expand_list[::-1]) * scale
    return (input_grads, reduce_grads, group_grads, expand_grads)
```

```python
import functools
import math

import jax
import jax.numpy as jnp
from jax import lax
from jax.experimental import pallas as pl
from jax.experimental.pallas import tpu as pltpu
from jax.sharding import PartitionSpec as P

imitation_weight = 0.5
tap_offsets = [(tap // 3 - 1, tap % 3 - 1) for tap in range(9)]
f32 = jnp.float32
bf16 = jnp.bfloat16


def dot_nn(a, b):
    return lax.dot_general(a, b, (((1,), (0,)), ((), ())), preferred_element_type=f32)


def dot_nt(a, b):
    return lax.dot_general(a, b, (((1,), (1,)), ((), ())), preferred_element_type=f32)


def dot_tn(a, b):
    return lax.dot_general(a, b, (((0,), (0,)), ((), ())), preferred_element_type=f32)


def kernel(
    dims,
    boxes_ref, counts_ref, bi_ref, out_ref, first_ref, second_ref, wr_ref, wg_ref, we_ref,
    wl_ref, teacher_ref, top_ref,
    grads_ref, reduce_ref, group_ref, expand_ref,
    inc, pas, wr_peer, dfx, ng, d_all, sec_all, bi_send, bi_all, ps_send, ps_all,
    gf, g_send, g_all, cnt, taps, ft,
    dp_send, dp_recv, core_send, core_recv, hop_send, hop_recv, fwd_send, fwd_recv,
):
    n, sections, crops, side, slots, pixels = dims
    rows, channels = bi_ref.shape
    half = channels // 2
    width = first_ref.shape[1]
    gw = wg_ref.shape[1]
    blk = taps.shape[2]
    blocks = width // blk
    cells = side * side
    share = channels // n
    k = gw // n
    hrows = rows // 2
    me = lax.axis_index("dp")
    s = lax.axis_index("section")
    c = lax.axis_index("chan")
    other = 1 - c
    last = sections - 1

    def remote(src, dst, send, recv, where):
        return pltpu.make_async_remote_copy(
            src_ref=src, dst_ref=dst, send_sem=send, recv_sem=recv,
            device_id=where, device_id_type=pl.DeviceIdType.MESH,
        )

    def dp_copies(what, src_of, dst):
        out = []
        for step in range(1, n):
            to = lax.rem(me + step, n)
            out.append(remote(src_of(to), dst, dp_send.at[what, step - 1],
                              dp_recv.at[what, step - 1], {"dp": to}))
        return out

    barrier = pltpu.get_barrier_semaphore()
    mesh_type = pl.DeviceIdType.MESH
    for step in range(1, n):
        pl.semaphore_signal(barrier, inc=1, device_id={"dp": lax.rem(me + step, n)},
                            device_id_type=mesh_type)
    pl.semaphore_signal(barrier, inc=1, device_id={"chan": other}, device_id_type=mesh_type)

    @pl.when(s > 0)
    def _():
        pl.semaphore_signal(barrier, inc=1, device_id={"section": s - 1},
                            device_id_type=mesh_type)

    @pl.when(s < last)
    def _():
        pl.semaphore_signal(barrier, inc=1, device_id={"section": s + 1},
                            device_id_type=mesh_type)

    row = lax.broadcasted_iota(jnp.int32, (cells, 128), 0)
    row_h, row_w = row // side, row % side
    masks = []
    for crop in range(crops):
        inside = jnp.zeros((cells, 128), f32)
        for r in range(slots):
            hit = ((row_h >= boxes_ref[crop, 4 * r]) & (row_h < boxes_ref[crop, 4 * r + 1])
                   & (row_w >= boxes_ref[crop, 4 * r + 2]) & (row_w < boxes_ref[crop, 4 * r + 3])
                   & (counts_ref[0, crop] > r))
            inside = jnp.where(hit, 1.0, inside)
        masks.append(inside)
    mask = jnp.concatenate(masks, axis=0)
    cnt[me] = jnp.broadcast_to(jnp.sum(mask, axis=0, keepdims=True), (8, 128))
    sec_all[me] = jnp.maximum(second_ref[...], 0)
    for j in range(n):
        bi_send[j] = bi_ref[:, j * share : (j + 1) * share]
    bi_all[me] = bi_send[me]

    pl.semaphore_wait(barrier, n + jnp.where(s > 0, 1, 0) + jnp.where(s < last, 1, 0))

    cnt_copies = dp_copies(0, lambda to: cnt.at[me], cnt.at[me])
    wr_copy = remote(wr_ref.at[pl.ds(pl.multiple_of(other * half, half), half)], wr_peer,
                     core_send.at[0], core_recv.at[0], {"chan": other})
    sec_copies = dp_copies(1, lambda to: sec_all.at[me], sec_all.at[me])
    bi_copies = dp_copies(2, lambda to: bi_send.at[to], bi_all.at[me])
    for copy in cnt_copies + [wr_copy] + sec_copies + bi_copies:
        copy.start()

    sel = (lax.broadcasted_iota(jnp.int32, (gw, blk), 1) % gw
           == lax.broadcasted_iota(jnp.int32, (gw, blk), 0)).astype(f32).astype(bf16)
    same = (lax.broadcasted_iota(jnp.int32, (blk, blk), 0) // gw
            == lax.broadcasted_iota(jnp.int32, (blk, blk), 1) // gw)
    for t in range(9):
        for b in range(blocks):
            base = t * width + b * blk
            dense = dot_nn(wg_ref[base : base + blk, :], sel)
            taps[t, b * blk : (b + 1) * blk, :] = jnp.where(same, dense, 0.0).astype(bf16)

    prow = lax.broadcasted_iota(jnp.int32, (rows, blk), 0)
    p_w = prow % side
    p_h = (prow // side) % side

    def h_ok(a):
        return p_h >= 1 if a == 1 else p_h < side - 1

    def w_ok(b):
        return p_w >= 1 if b == 1 else p_w < side - 1

    def moved(x, a, b):
        shift = (side * a + b) % rows
        if shift:
            x = pltpu.roll(x, shift, 0)
        if a:
            x = jnp.where(h_ok(a), x, 0.0)
        if b:
            x = jnp.where(w_ok(b), x, 0.0)
        return x

    def prepare_first():
        for b in range(blocks):
            first = jnp.maximum(first_ref[:, b * blk : (b + 1) * blk], 0).astype(f32)
            for t, (da, db) in enumerate(tap_offsets):
                ft[t, b] = moved(first, -da, -db).T.astype(bf16)

    hop_copies = [
        remote(ng.at[c, pl.ds(q * hrows, hrows)], inc.at[c, pl.ds(q * hrows, hrows)],
               hop_send.at[q], hop_recv.at[q], {"section": lax.max(s - 1, 0)})
        for q in range(2)
    ]
    fwd_copies = [
        remote(inc.at[c, pl.ds(q * hrows, hrows)], inc.at[c, pl.ds(q * hrows, hrows)],
               fwd_send.at[q], fwd_recv.at[q], {"chan": other})
        for q in range(2)
    ]

    @pl.when(s == last)
    def _():
        feature = jnp.maximum(out_ref[...], 0)
        lateral = dot_nn(feature, wl_ref[...])
        error = (mask[:, 0:1] * (lateral - teacher_ref[...].astype(f32))).astype(bf16)
        imitation = dot_nt(error, wl_ref[...])
        for copy in cnt_copies:
            copy.wait_recv()
        covered = cnt[0]
        for j in range(1, n):
            covered = covered + cnt[j]
        scale = (imitation_weight * pixels) / covered[0:1, 0:1]
        start = (top_ref[...].astype(f32) + imitation * scale).astype(bf16)
        start = jnp.where(out_ref[...] > 0, start, jnp.zeros_like(start))
        pas[0] = start[:, :half]
        pas[1] = start[:, half:]

    @pl.when(s < last)
    def _():
        for copy in cnt_copies:
            copy.wait_recv()
        prepare_first()
        for q in range(2):
            hop_copies[q].wait_recv()
            fwd_copies[q].start()
        for q in range(2):
            fwd_copies[q].wait_recv()
        for q in range(2):
            value = inc[q]
            gate = out_ref[:, q * half : (q + 1) * half] > 0
            pas[q] = jnp.where(gate, value, jnp.zeros_like(value))

    for j in range(n):
        lo = j * share
        q = lo // half
        ps_send[j] = pas[q, :, lo - q * half : lo - q * half + share]
    ps_all[me] = ps_send[me]
    ps_copies = dp_copies(3, lambda to: ps_send.at[to], ps_all.at[me])
    for copy in ps_copies:
        copy.start()

    second_full = dot_nt(pas[0], we_ref[:, :half]) + dot_nt(pas[1], we_ref[:, half:])
    d_second = jnp.where(second_ref[...] > 0, second_full, 0.0).astype(bf16)
    pieces = []
    for b in range(blocks):
        lhs = d_second[:, b * blk : (b + 1) * blk]
        total = None
        for db in (-1, 0, 1):
            column = None
            for da in (-1, 0, 1):
                t = 3 * (da + 1) + db + 1
                y = moved(dot_nt(lhs, taps[t, b * blk : (b + 1) * blk, :]), da, 0)
                column = y if column is None else column + y
            column = moved(column, 0, db)
            total = column if total is None else total + column
        pieces.append(jnp.where(first_ref[:, b * blk : (b + 1) * blk] > 0, total, 0.0).astype(bf16))
    d_first = jnp.concatenate(pieces, axis=1)
    d_all[me] = d_first

    dfx_copy = remote(d_all.at[me], dfx, core_send.at[1], core_recv.at[1], {"chan": other})
    dfx_copy.start()
    d_copies = dp_copies(4, lambda to: d_all.at[me], d_all.at[me])
    for copy in d_copies:
        copy.start()

    own_rows = pl.ds(pl.multiple_of(c * half, half), half)
    grad = dot_nt(d_first, wr_ref[own_rows, :]) + pas[c].astype(f32)
    wr_copy.wait_recv()
    dfx_copy.wait_recv()
    grad = grad + dot_nt(dfx[...], wr_peer[...])
    ng[c] = grad.astype(bf16)
    ng_copy = remote(ng.at[c], ng.at[c], core_send.at[2], core_recv.at[2], {"chan": other})

    @pl.when(s > 0)
    def _():
        for copy in hop_copies:
            copy.start()

    ng_copy.start()

    @pl.when(s == last)
    def _():
        prepare_first()

    gf[...] = jnp.zeros_like(gf)
    for b in range(blocks):
        rhs = d_second[:, b * blk : (b + 1) * blk]
        for t in range(9):
            dense = jnp.where(same, dot_nn(ft[t, b], rhs), 0.0)
            folded = jnp.sum(dense.reshape(blk // gw, gw, blk), axis=0)
            for j in range(n):
                gf[j, t * k : (t + 1) * k, b * blk : (b + 1) * blk] = folded[j * k : (j + 1) * k]
    g_send[...] = gf[...].astype(bf16)
    g_copies = dp_copies(5, lambda to: g_send.at[to], g_all.at[me])
    for copy in g_copies:
        copy.start()

    norm = 1.0 / math.sqrt(pixels)
    for copy in sec_copies + ps_copies:
        copy.wait_recv()
    expand = dot_tn(sec_all[...].reshape(n * rows, width), ps_all[...].reshape(n * rows, share))
    expand_ref[...] = expand * norm
    for copy in bi_copies + d_copies:
        copy.wait_recv()
    reduced = dot_tn(bi_all[...].reshape(n * rows, share), d_all[...].reshape(n * rows, width))
    reduce_ref[...] = reduced * norm
    for copy in g_copies:
        copy.wait_recv()
    g_all[me] = jnp.zeros(g_all.shape[1:], bf16)
    total = gf[me]
    for j in range(n):
        total = total + g_all[j].astype(f32)
    group_ref[...] = total * norm
    ng_copy.wait_recv()
    grads_ref[:, :half] = ng[0]
    grads_ref[:, half:] = ng[1]

    for copy in cnt_copies + sec_copies + bi_copies + ps_copies + d_copies + g_copies:
        copy.wait_send()
    for copy in (wr_copy, dfx_copy, ng_copy):
        copy.wait_send()

    @pl.when(s > 0)
    def _():
        for copy in hop_copies:
            copy.wait_send()

    @pl.when(s < last)
    def _():
        for copy in fwd_copies:
            copy.wait_send()


def on_device(
    block_inputs, out_pre, first_pre, second_pre, w_reduce, w_group, w_expand, w_lateral,
    teacher, top_grad, boxes, region_counts,
):
    n = lax.axis_size("dp")
    sections = lax.axis_size("section")
    crops, side, _, channels = top_grad.shape
    rows = crops * side * side
    width = first_pre.shape[4]
    lateral_width = w_lateral.shape[1]
    groups, gw = w_group.shape[2], w_group.shape[3]
    slots = boxes.shape[1]
    pixels = rows * n
    share = channels // n
    k = gw // n
    grows = -(-9 * k // 16) * 16
    half = channels // 2
    blk = min(256, width)
    vmem = pl.BlockSpec(memory_space=pltpu.VMEM)
    smem = pl.BlockSpec(memory_space=pltpu.SMEM)
    dma = pltpu.SemaphoreType.DMA
    peers = max(n - 1, 1)
    grads, reduced, group, expand = pl.pallas_call(
        functools.partial(kernel, (n, sections, crops, side, slots, pixels)),
        out_shape=(
            jax.ShapeDtypeStruct((rows, channels), bf16),
            jax.ShapeDtypeStruct((share, width), f32),
            jax.ShapeDtypeStruct((grows, width), f32),
            jax.ShapeDtypeStruct((width, share), f32),
        ),
        in_specs=[smem, smem] + [vmem] * 10,
        out_specs=(vmem,) * 4,
        scratch_shapes=[
            pltpu.VMEM((2, rows, half), bf16),
            pltpu.VMEM((2, rows, half), bf16),
            pltpu.VMEM((half, width), bf16),
            pltpu.VMEM((rows, width), bf16),
            pltpu.VMEM((2, rows, half), bf16),
            pltpu.VMEM((n, rows, width), bf16),
            pltpu.VMEM((n, rows, width), bf16),
            pltpu.VMEM((n, rows, share), bf16),
            pltpu.VMEM((n, rows, share), bf16),
            pltpu.VMEM((n, rows, share), bf16),
            pltpu.VMEM((n, rows, share), bf16),
            pltpu.VMEM((n, grows, width), f32),
            pltpu.VMEM((n, grows, width), bf16),
            pltpu.VMEM((n, grows, width), bf16),
            pltpu.VMEM((n, 8, 128), f32),
            pltpu.VMEM((9, width, blk), bf16),
            pltpu.VMEM((9, width // blk, blk, rows), bf16),
            dma((6, peers)), dma((6, peers)), dma((3,)), dma((3,)),
            dma((2,)), dma((2,)), dma((2,)), dma((2,)),
        ],
        compiler_params=pltpu.CompilerParams(
            collective_id=0, has_side_effects=True, vmem_limit_bytes=56 << 20,
        ),
    )(
        boxes.reshape(crops, slots * 4), region_counts.reshape(1, crops),
        block_inputs.reshape(rows, channels), out_pre.reshape(rows, channels),
        first_pre.reshape(rows, width), second_pre.reshape(rows, width),
        w_reduce[0], w_group.reshape(9 * groups * gw, gw), w_expand[0], w_lateral,
        teacher.reshape(rows, lateral_width), top_grad.reshape(rows, channels),
    )
    group = group[: 9 * k].reshape(9, k, groups, gw).transpose(0, 2, 1, 3)
    return (
        grads.reshape(1, crops, side, side, channels), reduced[None], group[None], expand[None],
    )


def solution(mesh):
    return jax.shard_map(
        on_device,
        mesh=mesh,
        in_specs=(
            P("section", ("parts", "dp"), None, None, None),
            P("section", ("parts", "dp"), None, None, None),
            P("section", ("parts", "dp"), None, None, "chan"),
            P("section", ("parts", "dp"), None, None, "chan"),
            P("section", None, "chan"),
            P("section", None, "chan", None, None),
            P("section", "chan", None),
            P(),
            P(("parts", "dp"), None, None, None),
            P(("parts", "dp"), None, None, None),
            P(("parts", "dp"), None, None),
            P(("parts", "dp")),
        ),
        out_specs=(
            P("section", ("parts", "dp"), None, None, None),
            P(("parts", "section"), "dp", "chan"),
            P(("parts", "section"), None, "chan", "dp", None),
            P(("parts", "section"), "chan", "dp"),
        ),
        check_vma=False,
    )
```

```python
import functools
import math

import jax
import jax.numpy as jnp
from jax import lax
from jax.experimental import pallas as pl
from jax.experimental.pallas import tpu as pltpu
from jax.sharding import PartitionSpec as P

imitation_weight = 0.5
tap_offsets = [(tap // 3 - 1, tap % 3 - 1) for tap in range(9)]
f32 = jnp.float32
bf16 = jnp.bfloat16


def dot_nn(a, b):
    return lax.dot_general(a, b, (((1,), (0,)), ((), ())), preferred_element_type=f32)


def dot_nt(a, b):
    return lax.dot_general(a, b, (((1,), (1,)), ((), ())), preferred_element_type=f32)


def dot_tn(a, b):
    return lax.dot_general(a, b, (((0,), (0,)), ((), ())), preferred_element_type=f32)


def kernel(
    dims,
    boxes_ref, counts_ref, bi_hbm, out_hbm, first_hbm, second_hbm, wr_hbm, wg_hbm, we_hbm,
    wl_hbm, teacher_hbm, top_hbm,
    grads_hbm, reduce_hbm, group_hbm, expand_hbm,
    bi_ref, out_ref, first_ref, second_ref, wr_ref, wg_ref, we_ref, wl_ref, teacher_ref, top_ref,
    reduce_ref, group_ref, expand_ref, load_sem, store_sem,
    inc, pas, wr_peer, dfx, ng, d_all, sec_all, bi_send, bi_all, ps_send, ps_all,
    gf, g_send, g_all, cnt, taps, ft,
    dp_send, dp_recv, core_send, core_recv, hop_send, hop_recv, fwd_send, fwd_recv,
    right_send, right_recv, left_send, left_recv, share_send, share_recv,
):
    n, sections, crops, side, slots, pixels = dims
    rows, channels = bi_ref.shape
    half = channels // 2
    width = first_ref.shape[1]
    groups = wg_ref.shape[1]
    gw = width // groups
    blk = taps.shape[2]
    blocks = width // blk
    cells = side * side
    share = channels // n
    k = gw // n
    hrows = rows // 2
    me = lax.axis_index("dp")
    s = lax.axis_index("section")
    c = lax.axis_index("chan")
    other = 1 - c
    last = sections - 1

    def remote(src, dst, send, recv, where):
        return pltpu.make_async_remote_copy(
            src_ref=src, dst_ref=dst, send_sem=send, recv_sem=recv,
            device_id=where, device_id_type=pl.DeviceIdType.MESH,
        )

    def dp_copies(what, src_of, dst):
        out = []
        for step in range(1, n):
            to = lax.rem(me + step, n)
            out.append(remote(src_of(to), dst, dp_send.at[what, step - 1],
                              dp_recv.at[what, step - 1], {"dp": to}))
        return out

    mine = pl.ds(pl.multiple_of(c * hrows, hrows), hrows)

    def share_copies(which, buf):
        out = []
        for step in range(1, n):
            rows_ref = buf.at[lax.rem(me + n - step, n), mine]
            out.append(remote(rows_ref, rows_ref, share_send.at[which, step - 1],
                              share_recv.at[which, step - 1], {"chan": other}))
        return out

    def line(step, buf):
        ahead, behind = buf.at[lax.max(me - step, 0)], buf.at[lax.min(me + step, n - 1)]
        right = remote(ahead, ahead, right_send.at[step], right_recv.at[step],
                       {"dp": lax.min(me + 1, n - 1)})
        left = remote(behind, behind, left_send.at[step], left_recv.at[step],
                      {"dp": lax.max(me - 1, 0)})
        return (
            (right, (me - step >= 0) & (me + 1 < n), me - 1 - step >= 0),
            (left, (me + step < n) & (me >= 1), me + 1 + step < n),
        )

    def line_start(moves):
        for copy, sends, _ in moves:
            pl.when(sends)(copy.start)

    def line_recv(moves):
        for copy, _, receives in moves:
            pl.when(receives)(copy.wait_recv)

    barrier = pltpu.get_barrier_semaphore()
    mesh_type = pl.DeviceIdType.MESH
    for step in range(1, n):
        pl.semaphore_signal(barrier, inc=1, device_id={"dp": lax.rem(me + step, n)},
                            device_id_type=mesh_type)
    pl.semaphore_signal(barrier, inc=1, device_id={"chan": other}, device_id_type=mesh_type)

    @pl.when(s > 0)
    def _():
        pl.semaphore_signal(barrier, inc=1, device_id={"section": s - 1},
                            device_id_type=mesh_type)

    @pl.when(s < last)
    def _():
        pl.semaphore_signal(barrier, inc=1, device_id={"section": s + 1},
                            device_id_type=mesh_type)

    pairs = [
        (second_hbm, second_ref), (bi_hbm, bi_ref), (wr_hbm, wr_ref), (out_hbm, out_ref),
        (wl_hbm, wl_ref), (teacher_hbm, teacher_ref), (top_hbm, top_ref), (we_hbm, we_ref),
        (wg_hbm, wg_ref), (first_hbm, first_ref),
    ]
    loads = [pltpu.make_async_copy(a, b, load_sem.at[i]) for i, (a, b) in enumerate(pairs)]
    for load in loads:
        load.start()

    row = lax.broadcasted_iota(jnp.int32, (cells, 128), 0)
    row_h, row_w = row // side, row % side
    masks = []
    for crop in range(crops):
        inside = jnp.zeros((cells, 128), f32)
        for r in range(slots):
            hit = ((row_h >= boxes_ref[crop, 0, r]) & (row_h < boxes_ref[crop, 1, r])
                   & (row_w >= boxes_ref[crop, 2, r]) & (row_w < boxes_ref[crop, 3, r])
                   & (counts_ref[0, crop] > r))
            inside = jnp.where(hit, 1.0, inside)
        masks.append(inside)
    mask = jnp.concatenate(masks, axis=0)
    cnt[me] = jnp.broadcast_to(jnp.sum(mask, axis=0, keepdims=True), (8, 128))
    loads[0].wait()
    loads[1].wait()
    loads[2].wait()
    sec_all[me] = jnp.maximum(second_ref[...], 0)
    for j in range(n):
        bi_send[j] = bi_ref[:, j * share : (j + 1) * share]
    bi_all[me] = bi_send[me]

    pl.semaphore_wait(barrier, n + jnp.where(s > 0, 1, 0) + jnp.where(s < last, 1, 0))

    cnt_copies = dp_copies(0, lambda to: cnt.at[me], cnt.at[me])
    wr_copy = remote(wr_ref.at[pl.ds(pl.multiple_of(other * half, half), half)], wr_peer,
                     core_send.at[0], core_recv.at[0], {"chan": other})
    sec_copies = dp_copies(1, lambda to: sec_all.at[me], sec_all.at[me])
    bi_copies = dp_copies(2, lambda to: bi_send.at[to, mine], bi_all.at[me, mine])
    for copy in cnt_copies + [wr_copy] + sec_copies + bi_copies:
        copy.start()

    loads[8].wait()
    pair = gw * gw
    iota = lambda shape, dim: lax.broadcasted_iota(jnp.int32, shape, dim)
    same = iota((blk, blk), 0) // gw == iota((blk, blk), 1) // gw
    same_out = iota((blk, pair), 0) % gw == iota((blk, pair), 1) % gw
    spread = (iota((pair, blk), 0) // gw == iota((pair, blk), 1) % gw).astype(f32).astype(bf16)
    for b in range(blocks):
        pick = (iota((blk, groups), 1) == b * (blk // gw) + iota((blk, groups), 0) // gw)
        pick = pick.astype(f32).astype(bf16)
        for t in range(9):
            values = dot_nt(pick, wg_ref[t * pair : (t + 1) * pair, :])
            values = jnp.where(same_out, values, 0.0).astype(bf16)
            dense = dot_nn(values, spread)
            taps[t, b * blk : (b + 1) * blk, :] = jnp.where(same, dense, 0.0).astype(bf16)

    prow = lax.broadcasted_iota(jnp.int32, (rows, blk), 0)
    p_w = prow % side
    p_h = (prow // side) % side

    def h_ok(a):
        return p_h >= 1 if a == 1 else p_h < side - 1

    def w_ok(b):
        return p_w >= 1 if b == 1 else p_w < side - 1

    def moved(x, a, b):
        shift = (side * a + b) % rows
        if shift:
            x = pltpu.roll(x, shift, 0)
        if a:
            x = jnp.where(h_ok(a), x, 0.0)
        if b:
            x = jnp.where(w_ok(b), x, 0.0)
        return x

    def prepare_first():
        for b in range(blocks):
            first = jnp.maximum(first_ref[:, b * blk : (b + 1) * blk], 0).astype(f32)
            for t, (da, db) in enumerate(tap_offsets):
                ft[t, b] = moved(first, -da, -db).T.astype(bf16)

    for i in (3, 4, 5, 6, 7, 9):
        loads[i].wait()

    hop_copies = [
        remote(ng.at[c, pl.ds(q * hrows, hrows)], inc.at[c, pl.ds(q * hrows, hrows)],
               hop_send.at[q], hop_recv.at[q], {"section": lax.max(s - 1, 0)})
        for q in range(2)
    ]
    fwd_copies = [
        remote(inc.at[c, pl.ds(q * hrows, hrows)], inc.at[c, pl.ds(q * hrows, hrows)],
               fwd_send.at[q], fwd_recv.at[q], {"chan": other})
        for q in range(2)
    ]

    @pl.when(s == last)
    def _():
        feature = jnp.maximum(out_ref[...], 0)
        lateral = dot_nn(feature, wl_ref[...])
        for copy in cnt_copies:
            copy.wait_recv()
        covered = cnt[0]
        for j in range(1, n):
            covered = covered + cnt[j]
        scale = (imitation_weight * pixels) / covered[0:1, 0:1]
        error = (mask[:, 0:1] * (lateral - teacher_ref[...].astype(f32)) * scale).astype(bf16)
        imitation = dot_nt(error, wl_ref[...])
        start = (top_ref[...].astype(f32) + imitation).astype(bf16)
        start = jnp.where(out_ref[...] > 0, start, jnp.zeros_like(start))
        pas[0] = start[:, :half]
        pas[1] = start[:, half:]

    @pl.when(s < last)
    def _():
        for copy in cnt_copies:
            copy.wait_recv()
        prepare_first()
        for q in range(2):
            hop_copies[q].wait_recv()
            fwd_copies[q].start()
        for q in range(2):
            fwd_copies[q].wait_recv()
        for q in range(2):
            value = inc[q]
            gate = out_ref[:, q * half : (q + 1) * half] > 0
            pas[q] = jnp.where(gate, value, jnp.zeros_like(value))

    for j in range(n):
        lo = j * share
        q = lo // half
        ps_send[j] = pas[q, :, lo - q * half : lo - q * half + share]
    ps_all[me] = ps_send[me]
    ps_copies = dp_copies(3, lambda to: ps_send.at[to, mine], ps_all.at[me, mine])
    for copy in ps_copies:
        copy.start()

    second_full = dot_nt(pas[0], we_ref[:, :half]) + dot_nt(pas[1], we_ref[:, half:])
    d_second = jnp.where(second_ref[...] > 0, second_full, 0.0).astype(bf16)
    pieces = []
    for b in range(blocks):
        lhs = d_second[:, b * blk : (b + 1) * blk]
        total = None
        for db in (-1, 0, 1):
            column = None
            for da in (-1, 0, 1):
                t = 3 * (da + 1) + db + 1
                y = moved(dot_nn(lhs, taps[t, b * blk : (b + 1) * blk, :]), da, 0)
                column = y if column is None else column + y
            column = moved(column, 0, db)
            total = column if total is None else total + column
        pieces.append(jnp.where(first_ref[:, b * blk : (b + 1) * blk] > 0, total, 0.0).astype(bf16))
    d_first = jnp.concatenate(pieces, axis=1)
    d_all[me] = d_first

    dfx_copy = remote(d_all.at[me], dfx, core_send.at[1], core_recv.at[1], {"chan": other})
    dfx_copy.start()
    moves = [line(step, d_all) for step in range(n - 1)]
    if moves:
        line_start(moves[0])

    own_rows = pl.ds(pl.multiple_of(c * half, half), half)
    grad = dot_nt(d_first, wr_ref[own_rows, :]) + pas[c].astype(f32)
    wr_copy.wait_recv()
    dfx_copy.wait_recv()
    grad = grad + dot_nt(dfx[...], wr_peer[...])
    ng[c] = grad.astype(bf16)
    ng_copy = remote(ng.at[c], ng.at[c], core_send.at[2], core_recv.at[2], {"chan": other})

    @pl.when(s > 0)
    def _():
        for copy in hop_copies:
            copy.start()

    ng_copy.start()

    @pl.when(s == last)
    def _():
        prepare_first()

    gf[...] = jnp.zeros_like(gf)
    for b in range(blocks):
        rhs = d_second[:, b * blk : (b + 1) * blk]
        for t in range(9):
            dense = jnp.where(same, dot_nn(ft[t, b], rhs), 0.0)
            folded = jnp.sum(dense.reshape(blk // gw, gw, blk), axis=0)
            for j in range(n):
                gf[j, t * k : (t + 1) * k, b * blk : (b + 1) * blk] = folded[j * k : (j + 1) * k]
    g_send[...] = gf[...].astype(bf16)
    g_copies = dp_copies(5, lambda to: g_send.at[to], g_all.at[me])
    for copy in g_copies:
        copy.start()

    norm = 1.0 / math.sqrt(pixels)
    bi_shares = share_copies(0, bi_all)
    ps_shares = share_copies(1, ps_all)
    for arrived, on in ((bi_copies, bi_shares), (ps_copies, ps_shares)):
        for copy, share_copy in zip(arrived, on):
            copy.wait_recv()
            share_copy.start()
    if len(moves) > 1:
        line_recv(moves[0])
        line_start(moves[1])
    ng_copy.wait_recv()
    stores = []
    for q in range(2):
        stores.append(pltpu.make_async_copy(
            ng.at[q], grads_hbm.at[:, q * half : (q + 1) * half], store_sem.at[q]))
        stores[q].start()
    for copy in sec_copies + ps_shares:
        copy.wait_recv()
    expand = dot_tn(sec_all[...].reshape(n * rows, width), ps_all[...].reshape(n * rows, share))
    expand_ref[...] = expand * norm
    stores.append(pltpu.make_async_copy(expand_ref, expand_hbm, store_sem.at[2]))
    stores[2].start()
    for copy in bi_shares:
        copy.wait_recv()
    for step in range(1, n - 1):
        line_recv(moves[step])
        if step + 1 < n - 1:
            line_start(moves[step + 1])
    if len(moves) == 1:
        line_recv(moves[0])
    reduced = dot_tn(bi_all[...].reshape(n * rows, share), d_all[...].reshape(n * rows, width))
    reduce_ref[...] = reduced * norm
    stores.append(pltpu.make_async_copy(reduce_ref, reduce_hbm, store_sem.at[3]))
    stores[3].start()
    for copy in g_copies:
        copy.wait_recv()
    g_all[me] = jnp.zeros(g_all.shape[1:], bf16)
    total = gf[me]
    for j in range(n):
        total = total + g_all[j].astype(f32)
    group_ref[...] = (total * norm)[: 9 * k]
    stores.append(pltpu.make_async_copy(group_ref, group_hbm, store_sem.at[4]))
    stores[4].start()
    for store in stores:
        store.wait()

    for moved_step in moves:
        for copy, sends, _ in moved_step:
            pl.when(sends)(copy.wait_send)
    for copy in bi_shares + ps_shares:
        copy.wait_send()
    for copy in cnt_copies + sec_copies + bi_copies + ps_copies + g_copies:
        copy.wait_send()
    for copy in (wr_copy, dfx_copy, ng_copy):
        copy.wait_send()

    @pl.when(s > 0)
    def _():
        for copy in hop_copies:
            copy.wait_send()

    @pl.when(s < last)
    def _():
        for copy in fwd_copies:
            copy.wait_send()


def on_device(
    block_inputs, out_pre, first_pre, second_pre, w_reduce, w_group, w_expand, w_lateral,
    teacher, top_grad, boxes, region_counts,
):
    n = lax.axis_size("dp")
    sections = lax.axis_size("section")
    crops, side, _, channels = top_grad.shape
    rows = crops * side * side
    width = first_pre.shape[4]
    lateral_width = w_lateral.shape[1]
    groups, gw = w_group.shape[2], w_group.shape[3]
    slots = boxes.shape[1]
    pixels = rows * n
    share = channels // n
    k = gw // n
    grows = -(-9 * k // 8) * 8
    half = channels // 2
    blk = min(256, width)
    hbm = pl.BlockSpec(memory_space=pl.ANY)
    smem = pl.BlockSpec(memory_space=pltpu.SMEM)
    dma = pltpu.SemaphoreType.DMA
    peers = max(n - 1, 1)
    grads, reduced, group, expand = pl.pallas_call(
        functools.partial(kernel, (n, sections, crops, side, slots, pixels)),
        out_shape=(
            jax.ShapeDtypeStruct((rows, channels), bf16),
            jax.ShapeDtypeStruct((share, width), f32),
            jax.ShapeDtypeStruct((9 * k, width), f32),
            jax.ShapeDtypeStruct((width, share), f32),
        ),
        in_specs=[smem, smem] + [hbm] * 10,
        out_specs=(hbm,) * 4,
        scratch_shapes=[
            pltpu.VMEM((rows, channels), bf16),
            pltpu.VMEM((rows, channels), bf16),
            pltpu.VMEM((rows, width), bf16),
            pltpu.VMEM((rows, width), bf16),
            pltpu.VMEM((channels, width), bf16),
            pltpu.VMEM((9 * gw * gw, groups), bf16),
            pltpu.VMEM((width, channels), bf16),
            pltpu.VMEM((channels, lateral_width), bf16),
            pltpu.VMEM((rows, lateral_width), bf16),
            pltpu.VMEM((rows, channels), bf16),
            pltpu.VMEM((share, width), f32),
            pltpu.VMEM((9 * k, width), f32),
            pltpu.VMEM((width, share), f32),
            dma((10,)), dma((5,)),
            pltpu.VMEM((2, rows, half), bf16),
            pltpu.VMEM((2, rows, half), bf16),
            pltpu.VMEM((half, width), bf16),
            pltpu.VMEM((rows, width), bf16),
            pltpu.VMEM((2, rows, half), bf16),
            pltpu.VMEM((n, rows, width), bf16),
            pltpu.VMEM((n, rows, width), bf16),
            pltpu.VMEM((n, rows, share), bf16),
            pltpu.VMEM((n, rows, share), bf16),
            pltpu.VMEM((n, rows, share), bf16),
            pltpu.VMEM((n, rows, share), bf16),
            pltpu.VMEM((n, grows, width), f32),
            pltpu.VMEM((n, grows, width), bf16),
            pltpu.VMEM((n, grows, width), bf16),
            pltpu.VMEM((n, 8, 128), f32),
            pltpu.VMEM((9, width, blk), bf16),
            pltpu.VMEM((9, width // blk, blk, rows), bf16),
            dma((6, peers)), dma((6, peers)), dma((3,)), dma((3,)),
            dma((2,)), dma((2,)), dma((2,)), dma((2,)),
            dma((peers,)), dma((peers,)), dma((peers,)), dma((peers,)), dma((2, peers)), dma((2, peers)),
        ],
        compiler_params=pltpu.CompilerParams(
            collective_id=0, has_side_effects=True, vmem_limit_bytes=56 << 20,
        ),
    )(
        boxes.transpose(0, 2, 1), region_counts.reshape(1, crops),
        block_inputs.reshape(rows, channels), out_pre.reshape(rows, channels),
        first_pre.reshape(rows, width), second_pre.reshape(rows, width),
        w_reduce[0], w_group[0].transpose(0, 2, 3, 1).reshape(9 * gw * gw, groups), w_expand[0], w_lateral,
        teacher.reshape(rows, lateral_width), top_grad.reshape(rows, channels),
    )
    group = group.reshape(9, k, groups, gw).transpose(0, 2, 1, 3)
    return (
        grads.reshape(1, crops, side, side, channels), reduced[None], group[None], expand[None],
    )


def solution(mesh):
    return jax.shard_map(
        on_device,
        mesh=mesh,
        in_specs=(
            P("section", ("parts", "dp"), None, None, None),
            P("section", ("parts", "dp"), None, None, None),
            P("section", ("parts", "dp"), None, None, "chan"),
            P("section", ("parts", "dp"), None, None, "chan"),
            P("section", None, "chan"),
            P("section", None, "chan", None, None),
            P("section", "chan", None),
            P(),
            P(("parts", "dp"), None, None, None),
            P(("parts", "dp"), None, None, None),
            P(("parts", "dp"), None, None),
            P(("parts", "dp")),
        ),
        out_specs=(
            P("section", ("parts", "dp"), None, None, None),
            P(("parts", "section"), "dp", "chan"),
            P(("parts", "section"), None, "chan", "dp", None),
            P(("parts", "section"), "chan", "dp"),
        ),
        check_vma=False,
    )
```

```python
import functools
import math

import jax
import jax.numpy as jnp
from jax import lax
from jax.experimental import pallas as pl
from jax.experimental.pallas import tpu as pltpu
from jax.sharding import PartitionSpec as P

imitation_weight = 0.5
tap_offsets = [(tap // 3 - 1, tap % 3 - 1) for tap in range(9)]
f32 = jnp.float32
bf16 = jnp.bfloat16


def dot_nn(a, b):
    return lax.dot_general(a, b, (((1,), (0,)), ((), ())), preferred_element_type=f32)


def dot_nt(a, b):
    return lax.dot_general(a, b, (((1,), (1,)), ((), ())), preferred_element_type=f32)


def dot_tn(a, b):
    return lax.dot_general(a, b, (((0,), (0,)), ((), ())), preferred_element_type=f32)


def kernel(
    dims,
    boxes_ref, counts_ref, bi_hbm, out_hbm, first_hbm, second_hbm, wr_hbm, wg_hbm, we_hbm,
    wl_hbm, teacher_hbm, top_hbm,
    grads_hbm, reduce_hbm, group_hbm, expand_hbm,
    bi_ref, out_ref, first_ref, second_ref, wr_ref, wg_ref, we_ref, wl_ref, teacher_ref, top_ref,
    reduce_ref, group_ref, expand_ref, load_sem, store_sem,
    inc, pas, wr_peer, dfx, ng, d_all, sec_all, bi_send, bi_all, ps_send, ps_all,
    gf, g_send, g_all, cnt, taps, ft,
    dp_send, dp_recv, core_send, core_recv, hop_send, hop_recv, fwd_send, fwd_recv,
    right_send, right_recv, left_send, left_recv, share_send, share_recv,
):
    n, sections, crops, side, slots, pixels = dims
    rows, channels = bi_ref.shape
    half = channels // 2
    width = first_ref.shape[1]
    groups = wg_ref.shape[1]
    gw = width // groups
    blk = taps.shape[2]
    blocks = width // blk
    cells = side * side
    share = channels // n
    k = gw // n
    hrows = rows // 2
    me = lax.axis_index("dp")
    s = lax.axis_index("section")
    c = lax.axis_index("chan")
    other = 1 - c
    last = sections - 1

    def remote(src, dst, send, recv, where):
        return pltpu.make_async_remote_copy(
            src_ref=src, dst_ref=dst, send_sem=send, recv_sem=recv,
            device_id=where, device_id_type=pl.DeviceIdType.MESH,
        )

    def dp_copies(what, src_of, dst):
        out = []
        for step in range(1, n):
            to = lax.rem(me + step, n)
            out.append(remote(src_of(to), dst, dp_send.at[what, step - 1],
                              dp_recv.at[what, step - 1], {"dp": to}))
        return out

    mine = pl.ds(pl.multiple_of(c * hrows, hrows), hrows)

    def share_copies(which, buf):
        out = []
        for step in range(1, n):
            rows_ref = buf.at[lax.rem(me + n - step, n), mine]
            out.append(remote(rows_ref, rows_ref, share_send.at[which, step - 1],
                              share_recv.at[which, step - 1], {"chan": other}))
        return out

    def line(step, q, buf):
        part = pl.ds(q * hrows, hrows)
        ahead = buf.at[lax.max(me - step, 0), part]
        behind = buf.at[lax.min(me + step, n - 1), part]
        right = remote(ahead, ahead, right_send.at[step, q], right_recv.at[step, q],
                       {"dp": lax.min(me + 1, n - 1)})
        left = remote(behind, behind, left_send.at[step, q], left_recv.at[step, q],
                      {"dp": lax.max(me - 1, 0)})
        return (
            (right, (me - step >= 0) & (me + 1 < n), me - 1 - step >= 0),
            (left, (me + step < n) & (me >= 1), me + 1 + step < n),
        )

    def line_start(moves):
        for copy, sends, _ in moves:
            pl.when(sends)(copy.start)

    def line_recv(moves):
        for copy, _, receives in moves:
            pl.when(receives)(copy.wait_recv)

    barrier = pltpu.get_barrier_semaphore()
    mesh_type = pl.DeviceIdType.MESH
    for step in range(1, n):
        pl.semaphore_signal(barrier, inc=1, device_id={"dp": lax.rem(me + step, n)},
                            device_id_type=mesh_type)
    pl.semaphore_signal(barrier, inc=1, device_id={"chan": other}, device_id_type=mesh_type)

    @pl.when(s > 0)
    def _():
        pl.semaphore_signal(barrier, inc=1, device_id={"section": s - 1},
                            device_id_type=mesh_type)

    @pl.when(s < last)
    def _():
        pl.semaphore_signal(barrier, inc=1, device_id={"section": s + 1},
                            device_id_type=mesh_type)

    pairs = [
        (second_hbm, second_ref), (bi_hbm, bi_ref), (wr_hbm, wr_ref), (out_hbm, out_ref),
        (wl_hbm, wl_ref), (teacher_hbm, teacher_ref), (top_hbm, top_ref), (we_hbm, we_ref),
        (wg_hbm, wg_ref), (first_hbm, first_ref),
    ]
    loads = [pltpu.make_async_copy(a, b, load_sem.at[i]) for i, (a, b) in enumerate(pairs)]
    for load in loads:
        load.start()

    row = lax.broadcasted_iota(jnp.int32, (cells, 128), 0)
    row_h, row_w = row // side, row % side
    masks = []
    for crop in range(crops):
        inside = jnp.zeros((cells, 128), f32)
        for r in range(slots):
            hit = ((row_h >= boxes_ref[crop, 0, r]) & (row_h < boxes_ref[crop, 1, r])
                   & (row_w >= boxes_ref[crop, 2, r]) & (row_w < boxes_ref[crop, 3, r])
                   & (counts_ref[0, crop] > r))
            inside = jnp.where(hit, 1.0, inside)
        masks.append(inside)
    mask = jnp.concatenate(masks, axis=0)
    cnt[me] = jnp.broadcast_to(jnp.sum(mask, axis=0, keepdims=True), (8, 128))
    loads[0].wait()
    loads[1].wait()
    loads[2].wait()
    sec_all[me] = jnp.maximum(second_ref[...], 0)
    for j in range(n):
        bi_send[j] = bi_ref[:, j * share : (j + 1) * share]
    bi_all[me] = bi_send[me]

    pl.semaphore_wait(barrier, n + jnp.where(s > 0, 1, 0) + jnp.where(s < last, 1, 0))

    cnt_copies = dp_copies(0, lambda to: cnt.at[me], cnt.at[me])
    wr_copy = remote(wr_ref.at[pl.ds(pl.multiple_of(other * half, half), half)], wr_peer,
                     core_send.at[0], core_recv.at[0], {"chan": other})
    sec_copies = dp_copies(1, lambda to: sec_all.at[me], sec_all.at[me])
    bi_copies = dp_copies(2, lambda to: bi_send.at[to, mine], bi_all.at[me, mine])
    for copy in cnt_copies + [wr_copy] + sec_copies + bi_copies:
        copy.start()

    loads[8].wait()
    pair = gw * gw
    iota = lambda shape, dim: lax.broadcasted_iota(jnp.int32, shape, dim)
    same = iota((blk, blk), 0) // gw == iota((blk, blk), 1) // gw
    same_out = iota((blk, pair), 0) % gw == iota((blk, pair), 1) % gw
    spread = (iota((pair, blk), 0) // gw == iota((pair, blk), 1) % gw).astype(f32).astype(bf16)
    for b in range(blocks):
        pick = (iota((blk, groups), 1) == b * (blk // gw) + iota((blk, groups), 0) // gw)
        pick = pick.astype(f32).astype(bf16)
        for t in range(9):
            values = dot_nt(pick, wg_ref[t * pair : (t + 1) * pair, :])
            values = jnp.where(same_out, values, 0.0).astype(bf16)
            dense = dot_nn(values, spread)
            taps[t, b * blk : (b + 1) * blk, :] = jnp.where(same, dense, 0.0).astype(bf16)

    prow = lax.broadcasted_iota(jnp.int32, (rows, blk), 0)
    p_w = prow % side
    p_h = (prow // side) % side

    def h_ok(a):
        return p_h >= 1 if a == 1 else p_h < side - 1

    def w_ok(b):
        return p_w >= 1 if b == 1 else p_w < side - 1

    def moved(x, a, b):
        shift = (side * a + b) % rows
        if shift:
            x = pltpu.roll(x, shift, 0)
        if a:
            x = jnp.where(h_ok(a), x, 0.0)
        if b:
            x = jnp.where(w_ok(b), x, 0.0)
        return x

    def prepare_first():
        for b in range(blocks):
            first = jnp.maximum(first_ref[:, b * blk : (b + 1) * blk], 0).astype(f32)
            for t, (da, db) in enumerate(tap_offsets):
                ft[t, b] = moved(first, -da, -db).T.astype(bf16)

    for i in (3, 4, 5, 6, 7, 9):
        loads[i].wait()

    hop_copies = [
        remote(ng.at[c, pl.ds(q * hrows, hrows)], inc.at[c, pl.ds(q * hrows, hrows)],
               hop_send.at[q], hop_recv.at[q], {"section": lax.max(s - 1, 0)})
        for q in range(2)
    ]
    fwd_copies = [
        remote(inc.at[c, pl.ds(q * hrows, hrows)], inc.at[c, pl.ds(q * hrows, hrows)],
               fwd_send.at[q], fwd_recv.at[q], {"chan": other})
        for q in range(2)
    ]

    @pl.when(s == last)
    def _():
        feature = jnp.maximum(out_ref[...], 0)
        lateral = dot_nn(feature, wl_ref[...])
        for copy in cnt_copies:
            copy.wait_recv()
        covered = cnt[0]
        for j in range(1, n):
            covered = covered + cnt[j]
        scale = (imitation_weight * pixels) / covered[0:1, 0:1]
        error = (mask[:, 0:1] * (lateral - teacher_ref[...].astype(f32)) * scale).astype(bf16)
        imitation = dot_nt(error, wl_ref[...])
        start = (top_ref[...].astype(f32) + imitation).astype(bf16)
        start = jnp.where(out_ref[...] > 0, start, jnp.zeros_like(start))
        pas[0] = start[:, :half]
        pas[1] = start[:, half:]

    @pl.when(s < last)
    def _():
        prepare_first()
        for q in range(2):
            hop_copies[q].wait_recv()
            fwd_copies[q].start()
        for q in range(2):
            fwd_copies[q].wait_recv()
        for q in range(2):
            value = inc[q]
            gate = out_ref[:, q * half : (q + 1) * half] > 0
            pas[q] = jnp.where(gate, value, jnp.zeros_like(value))

    for j in range(n):
        lo = j * share
        q = lo // half
        ps_send[j] = pas[q, :, lo - q * half : lo - q * half + share]
    ps_all[me] = ps_send[me]
    ps_copies = dp_copies(3, lambda to: ps_send.at[to, mine], ps_all.at[me, mine])
    for copy in ps_copies:
        copy.start()

    second_full = dot_nt(pas[0], we_ref[:, :half]) + dot_nt(pas[1], we_ref[:, half:])
    d_second = jnp.where(second_ref[...] > 0, second_full, 0.0).astype(bf16)
    pieces = []
    for b in range(blocks):
        lhs = d_second[:, b * blk : (b + 1) * blk]
        total = None
        for db in (-1, 0, 1):
            column = None
            for da in (-1, 0, 1):
                t = 3 * (da + 1) + db + 1
                y = moved(dot_nn(lhs, taps[t, b * blk : (b + 1) * blk, :]), da, 0)
                column = y if column is None else column + y
            column = moved(column, 0, db)
            total = column if total is None else total + column
        pieces.append(jnp.where(first_ref[:, b * blk : (b + 1) * blk] > 0, total, 0.0).astype(bf16))
    d_first = jnp.concatenate(pieces, axis=1)
    d_all[me] = d_first

    dfx_copy = remote(d_all.at[me], dfx, core_send.at[1], core_recv.at[1], {"chan": other})
    dfx_copy.start()
    moves = [[line(step, q, d_all) for q in range(2)] for step in range(n - 1)]
    for move in moves[:1]:
        line_start(move[0])
        line_start(move[1])

    own_rows = pl.ds(pl.multiple_of(c * half, half), half)
    grad = dot_nt(d_first, wr_ref[own_rows, :]) + pas[c].astype(f32)
    wr_copy.wait_recv()
    dfx_copy.wait_recv()
    grad = grad + dot_nt(dfx[...], wr_peer[...])
    ng[c] = grad.astype(bf16)
    ng_copy = remote(ng.at[c], ng.at[c], core_send.at[2], core_recv.at[2], {"chan": other})

    @pl.when(s > 0)
    def _():
        for copy in hop_copies:
            copy.start()

    ng_copy.start()

    @pl.when(s == last)
    def _():
        prepare_first()

    gf[...] = jnp.zeros_like(gf)
    for b in range(blocks):
        rhs = d_second[:, b * blk : (b + 1) * blk]
        for t in range(9):
            dense = jnp.where(same, dot_nn(ft[t, b], rhs), 0.0)
            folded = jnp.sum(dense.reshape(blk // gw, gw, blk), axis=0)
            for j in range(n):
                gf[j, t * k : (t + 1) * k, b * blk : (b + 1) * blk] = folded[j * k : (j + 1) * k]
    g_send[...] = gf[...].astype(bf16)
    g_copies = dp_copies(5, lambda to: g_send.at[to], g_all.at[me])
    for copy in g_copies:
        copy.start()

    norm = 1.0 / math.sqrt(pixels)
    bi_shares = share_copies(0, bi_all)
    ps_shares = share_copies(1, ps_all)
    for arrived, on in ((bi_copies, bi_shares), (ps_copies, ps_shares)):
        for copy, share_copy in zip(arrived, on):
            copy.wait_recv()
            share_copy.start()
    if len(moves) > 1:
        for q in range(2):
            line_recv(moves[0][q])
            line_start(moves[1][q])
    ng_copy.wait_recv()
    stores = []
    for q in range(2):
        stores.append(pltpu.make_async_copy(
            ng.at[q], grads_hbm.at[:, q * half : (q + 1) * half], store_sem.at[q]))
        stores[q].start()
    for copy in sec_copies + ps_shares:
        copy.wait_recv()
    expand = dot_tn(sec_all[...].reshape(n * rows, width), ps_all[...].reshape(n * rows, share))
    expand_ref[...] = expand * norm
    stores.append(pltpu.make_async_copy(expand_ref, expand_hbm, store_sem.at[2]))
    stores[2].start()
    for copy in bi_shares:
        copy.wait_recv()
    for step in range(1, n - 1):
        for q in range(2):
            line_recv(moves[step][q])
            if step + 1 < n - 1:
                line_start(moves[step + 1][q])
    if len(moves) == 1:
        for q in range(2):
            line_recv(moves[0][q])
    reduced = dot_tn(bi_all[...].reshape(n * rows, share), d_all[...].reshape(n * rows, width))
    reduce_ref[...] = reduced * norm
    stores.append(pltpu.make_async_copy(reduce_ref, reduce_hbm, store_sem.at[3]))
    stores[3].start()
    for copy in g_copies:
        copy.wait_recv()
    g_all[me] = jnp.zeros(g_all.shape[1:], bf16)
    total = gf[me]
    for j in range(n):
        total = total + g_all[j].astype(f32)
    group_ref[...] = (total * norm)[: 9 * k]
    stores.append(pltpu.make_async_copy(group_ref, group_hbm, store_sem.at[4]))
    stores[4].start()
    for store in stores:
        store.wait()

    @pl.when(s < last)
    def _():
        for copy in cnt_copies:
            copy.wait_recv()

    for moved_step in moves:
        for move in moved_step:
            for copy, sends, _ in move:
                pl.when(sends)(copy.wait_send)
    for copy in bi_shares + ps_shares:
        copy.wait_send()
    for copy in cnt_copies + sec_copies + bi_copies + ps_copies + g_copies:
        copy.wait_send()
    for copy in (wr_copy, dfx_copy, ng_copy):
        copy.wait_send()

    @pl.when(s > 0)
    def _():
        for copy in hop_copies:
            copy.wait_send()

    @pl.when(s < last)
    def _():
        for copy in fwd_copies:
            copy.wait_send()


def on_device(
    block_inputs, out_pre, first_pre, second_pre, w_reduce, w_group, w_expand, w_lateral,
    teacher, top_grad, boxes, region_counts,
):
    n = lax.axis_size("dp")
    sections = lax.axis_size("section")
    crops, side, _, channels = top_grad.shape
    rows = crops * side * side
    width = first_pre.shape[4]
    lateral_width = w_lateral.shape[1]
    groups, gw = w_group.shape[2], w_group.shape[3]
    slots = boxes.shape[1]
    pixels = rows * n
    share = channels // n
    k = gw // n
    grows = -(-9 * k // 8) * 8
    half = channels // 2
    blk = min(256, width)
    hbm = pl.BlockSpec(memory_space=pl.ANY)
    smem = pl.BlockSpec(memory_space=pltpu.SMEM)
    dma = pltpu.SemaphoreType.DMA
    peers = max(n - 1, 1)
    grads, reduced, group, expand = pl.pallas_call(
        functools.partial(kernel, (n, sections, crops, side, slots, pixels)),
        out_shape=(
            jax.ShapeDtypeStruct((rows, channels), bf16),
            jax.ShapeDtypeStruct((share, width), f32),
            jax.ShapeDtypeStruct((9 * k, width), f32),
            jax.ShapeDtypeStruct((width, share), f32),
        ),
        in_specs=[smem, smem] + [hbm] * 10,
        out_specs=(hbm,) * 4,
        scratch_shapes=[
            pltpu.VMEM((rows, channels), bf16),
            pltpu.VMEM((rows, channels), bf16),
            pltpu.VMEM((rows, width), bf16),
            pltpu.VMEM((rows, width), bf16),
            pltpu.VMEM((channels, width), bf16),
            pltpu.VMEM((9 * gw * gw, groups), bf16),
            pltpu.VMEM((width, channels), bf16),
            pltpu.VMEM((channels, lateral_width), bf16),
            pltpu.VMEM((rows, lateral_width), bf16),
            pltpu.VMEM((rows, channels), bf16),
            pltpu.VMEM((share, width), f32),
            pltpu.VMEM((9 * k, width), f32),
            pltpu.VMEM((width, share), f32),
            dma((10,)), dma((5,)),
            pltpu.VMEM((2, rows, half), bf16),
            pltpu.VMEM((2, rows, half), bf16),
            pltpu.VMEM((half, width), bf16),
            pltpu.VMEM((rows, width), bf16),
            pltpu.VMEM((2, rows, half), bf16),
            pltpu.VMEM((n, rows, width), bf16),
            pltpu.VMEM((n, rows, width), bf16),
            pltpu.VMEM((n, rows, share), bf16),
            pltpu.VMEM((n, rows, share), bf16),
            pltpu.VMEM((n, rows, share), bf16),
            pltpu.VMEM((n, rows, share), bf16),
            pltpu.VMEM((n, grows, width), f32),
            pltpu.VMEM((n, grows, width), bf16),
            pltpu.VMEM((n, grows, width), bf16),
            pltpu.VMEM((n, 8, 128), f32),
            pltpu.VMEM((9, width, blk), bf16),
            pltpu.VMEM((9, width // blk, blk, rows), bf16),
            dma((6, peers)), dma((6, peers)), dma((3,)), dma((3,)),
            dma((2,)), dma((2,)), dma((2,)), dma((2,)),
            dma((peers, 2)), dma((peers, 2)), dma((peers, 2)), dma((peers, 2)), dma((2, peers)), dma((2, peers)),
        ],
        compiler_params=pltpu.CompilerParams(
            collective_id=0, has_side_effects=True, vmem_limit_bytes=56 << 20,
        ),
    )(
        boxes.transpose(0, 2, 1), region_counts.reshape(1, crops),
        block_inputs.reshape(rows, channels), out_pre.reshape(rows, channels),
        first_pre.reshape(rows, width), second_pre.reshape(rows, width),
        w_reduce[0], w_group[0].transpose(0, 2, 3, 1).reshape(9 * gw * gw, groups), w_expand[0], w_lateral,
        teacher.reshape(rows, lateral_width), top_grad.reshape(rows, channels),
    )
    group = group.reshape(9, k, groups, gw).transpose(0, 2, 1, 3)
    return (
        grads.reshape(1, crops, side, side, channels), reduced[None], group[None], expand[None],
    )


def solution(mesh):
    return jax.shard_map(
        on_device,
        mesh=mesh,
        in_specs=(
            P("section", ("parts", "dp"), None, None, None),
            P("section", ("parts", "dp"), None, None, None),
            P("section", ("parts", "dp"), None, None, "chan"),
            P("section", ("parts", "dp"), None, None, "chan"),
            P("section", None, "chan"),
            P("section", None, "chan", None, None),
            P("section", "chan", None),
            P(),
            P(("parts", "dp"), None, None, None),
            P(("parts", "dp"), None, None, None),
            P(("parts", "dp"), None, None),
            P(("parts", "dp")),
        ),
        out_specs=(
            P("section", ("parts", "dp"), None, None, None),
            P(("parts", "section"), "dp", "chan"),
            P(("parts", "section"), None, "chan", "dp", None),
            P(("parts", "section"), "chan", "dp"),
        ),
        check_vma=False,
    )
```
